32 devices in a mesh: year: 4 (over x, core), date: 4 (over z), pix: 2 (over y).
Axes of the slice: x: 2, y: 2, z: 4, core: 2. Of those that a mesh axis runs over, the one named last changes fastest.
Arguments:
- predicted_anomaly: bfloat16 [8, 4, 4, 83, 16384], P('year', 'date', None, None, 'pix'), may hold values from -6 to 6
- measured_anomaly: bfloat16 [8, 4, 4, 83, 16384], P('year', 'date', None, None, 'pix'), may hold values from -6 to 6
- filled_calendar: int32 [4], P('date'), may hold values from 1 to 4, 10 in all
Outputs:
- mean_error_field: float32 [4, 83, 2, 8192], P('date', None, 'pix', 'year')
- acc_map: float32 [83, 2, 8192], P(None, 'pix', ('year', 'date'))
- rmse_map: float32 [83, 2, 8192], P(None, 'pix', ('year', 'date'))
- scores: float32 [2, 83], replicated
The draws below stay inside these ranges and needn't reach their ends.
Inputs may be any that keep to these rules, and one draw needn't show every extreme that they name: `filled_calendar`: counts sum to 10, and some window uses all 4 slots.
All inputs are finite; a program needn't handle non-finite values. No bound on the sum of `filled_calendar` on one device may be relied on, other than what follows from the above.
Results may differ from the reference program's by a relative error of at most 0.0003.
Values sent between devices are 32-bit elements; how exact they have to be, the bound alone decides.
No kernel may reach another device: no remote copies, remote signals or barrier semaphores. Data moves between devices by JAX's collectives and lax.ppermute only.
A program may use at most 128 MiB of HBM per device.

```python
import math
import jax
import jax.numpy as jnp
import numpy as np
from jax import lax

NUM_VARIABLES = 83
P_DEV = 8192
CALENDAR_SPOTS = 4
HINDCAST_SPAN = 8
SEASON_SPANS = 4
GRID_POINTS = 16384
N_PIX = 2


def levels(key, dims, shards, least, high):
    gain = 1.0
    for position, shards_of in shards:
        heights = jax.random.uniform(jax.random.fold_in(jax.random.fold_in(key, 6), position), (shards_of,), jnp.float32, least / len(shards), high / len(shards))
        gain = gain * jnp.repeat(jnp.exp(heights), dims[position] // shards_of).reshape((-1,) + (1,) * (len(dims) - 1 - position))
    return gain


def profile(count, total, limit, lean):
    weights = [(1 << 20) // math.isqrt(rank ** lean) + 1 for rank in range(2, count + 1)]
    rest, given = total - limit - (count - 1), [1] * (count - 1)
    while rest > 0:
        free = [i for i in range(count - 1) if given[i] < limit]
        pool, left = sum([weights[i] for i in free]), rest
        for i in free:
            addition = min(limit - given[i], max(1, left * weights[i] // pool), rest)
            given[i] = given[i] + addition
            rest = rest - addition
    return np.array([limit] + given)


def ragged(key, count, total, limit, slope):
    if count == 2:
        one = jax.random.randint(key, (), max(1, total - limit), min(limit, total - 1) + 1)
        return jnp.stack([one, total - one])
    tallies = jnp.asarray(profile(count, total, limit, slope), jnp.int32)
    pairs = (count - 1) // 2
    donor, receiver = tallies[1:1 + 2 * pairs:2], tallies[2:2 + 2 * pairs:2]
    margin = jnp.minimum(donor - 1, limit - receiver)
    shifted = jax.random.randint(jax.random.fold_in(key, 1), (pairs,), 0, 1 << 20) % (margin + 1)
    tallies = tallies.at[1:1 + 2 * pairs:2].set(donor - shifted).at[2:2 + 2 * pairs:2].set(receiver + shifted)
    return tallies[jax.random.permutation(jax.random.fold_in(key, 2), count)]


def gaussian(own_key, dims, scale, most, cuts=(), kind=jnp.bfloat16):
    values = scale * jax.random.normal(own_key, dims, jnp.float32)
    if cuts:
        values = values * levels(own_key, dims, cuts, -0.22, 0.18)
    return jnp.clip(values, -most, most).astype(kind)


def setup_inputs(seed: int = 0) -> dict:
    seeds = jax.random.split(jax.random.key(seed), 4)
    return {
        "predicted_anomaly": gaussian(seeds[0], (HINDCAST_SPAN, SEASON_SPANS, CALENDAR_SPOTS, NUM_VARIABLES, GRID_POINTS), 1.0, 6.0, ((0, 4), (1, 4), (4, 2))),
        "measured_anomaly": gaussian(seeds[1], (HINDCAST_SPAN, SEASON_SPANS, CALENDAR_SPOTS, NUM_VARIABLES, GRID_POINTS), 1.0, 6.0, ((0, 4), (1, 4), (4, 2))),
        "filled_calendar": ragged(seeds[2], SEASON_SPANS, 5 * SEASON_SPANS // 2, CALENDAR_SPOTS, 0).astype(jnp.int32),
    }


def reference(predicted_anomaly, measured_anomaly, filled_calendar):
    grid_extent = predicted_anomaly.shape[-1]
    variable_group = predicted_anomaly.shape[3]
    zero = jnp.zeros((variable_group, grid_extent), jnp.float32)
    s_fo, s_ff, s_oo, s_ee = (zero, zero, zero, zero)
    biases = []
    for season_number in range(SEASON_SPANS):
        predicted_season = predicted_anomaly[:, season_number].astype(jnp.float32)
        measured_season = measured_anomaly[:, season_number].astype(jnp.float32)
        valid = (jnp.arange(CALENDAR_SPOTS, dtype=jnp.int32) < filled_calendar[season_number]).astype(jnp.float32)[None, :, None, None]
        error_field = predicted_season - measured_season
        mean_error_field = lax.optimization_barrier(jnp.sum(valid * error_field, axis=(0, 1))) / (HINDCAST_SPAN * filled_calendar[season_number].astype(jnp.float32))
        biases.append(mean_error_field)
        corrected_anomaly = predicted_season - mean_error_field
        s_fo = s_fo + lax.optimization_barrier(jnp.sum(valid * corrected_anomaly * measured_season, axis=(0, 1)))
        s_ff = s_ff + lax.optimization_barrier(jnp.sum(valid * corrected_anomaly * corrected_anomaly, axis=(0, 1)))
        s_oo = s_oo + lax.optimization_barrier(jnp.sum(valid * measured_season * measured_season, axis=(0, 1)))
        spread = corrected_anomaly - measured_season
        s_ee = s_ee + lax.optimization_barrier(jnp.sum(valid * spread * spread, axis=(0, 1)))
    samples = HINDCAST_SPAN * jnp.sum(filled_calendar).astype(jnp.float32)
    acc = s_fo / jnp.sqrt(s_ff * s_oo + 1e-06)
    rmse = jnp.sqrt(s_ee / samples)
    rows = (jnp.arange(grid_extent, dtype=jnp.int32) % 181 - 90).astype(jnp.float32)
    lat_weight = jnp.cos(rows * (math.pi / 180.0))
    numer = jnp.stack([lax.optimization_barrier(jnp.sum(acc * lat_weight, axis=1)), lax.optimization_barrier(jnp.sum(rmse * lat_weight, axis=1))])
    scores = numer / jnp.sum(lat_weight)
    bias_out = jnp.stack(biases).reshape(SEASON_SPANS, variable_group, N_PIX, P_DEV)
    return (bias_out, acc.reshape(variable_group, N_PIX, P_DEV), rmse.reshape(variable_group, N_PIX, P_DEV), scores)
```

```python
import functools
import math

import jax
import jax.numpy as jnp
from jax import lax
from jax.experimental import pallas as pl
from jax.experimental.pallas import tpu as pltpu
from jax.sharding import PartitionSpec as P


LANES = 128
CORES = 2
BLOCK = 8
STEP = 32
FIELDS = 5
CROSS = 4
SPLITS = (40,)


def moments_kernel(chips, dates, tiles, slots, where_ref, f_ref, o_ref, keep_ref, send_ref, acc_ref):
    years = f_ref.shape[0]
    per_channel = chips * CORES * dates * tiles * slots
    group = max(1, 8 // tiles)
    count, core, chip = where_ref[0], where_ref[1], where_ref[2]
    used = [(s < count).astype(jnp.float32) for s in range(slots)]
    piece = min(8, dates * tiles)

    @pl.loop(0, BLOCK // group)
    def _(g):
        for i in range(group):
            base = pl.multiple_of((g * group + i) * per_channel, per_channel)
            for sub in range(0, per_channel, STEP):
                sums = None
                for y in range(years):
                    f = f_ref[y, pl.ds(base + sub, STEP), :].astype(jnp.float32)
                    o = o_ref[y, pl.ds(base + sub, STEP), :].astype(jnp.float32)
                    terms = (f - o, o, f * f, f * o, o * o)
                    sums = terms if sums is None else tuple(a + b for a, b in zip(sums, terms))
                for field in range(FIELDS):
                    acc_ref[field, i * per_channel + sub : i * per_channel + sub + STEP, :] = sums[field]
        for c in range(CORES):
            out_ref = (keep_ref, send_ref)[c]
            for x in range(chips):
                block = lax.rem(chip + x, chips) * CORES + lax.rem(core + c, CORES)
                for i in range(group):
                    row = pl.multiple_of(g * (group * tiles), group * tiles) + i * tiles
                    for p in range(0, dates * tiles, piece):
                        start = block * (dates * tiles * slots) + (i * per_channel + p * slots)
                        for field in range(FIELDS):
                            total = None
                            for s in range(slots):
                                v = acc_ref[field, pl.ds(start + s, piece, stride=slots), :] * used[s]
                                total = v if total is None else total + v
                            for j in range(piece // tiles):
                                out_ref[field, x, p // tiles + j, pl.ds(row, tiles), :] = total[
                                    j * tiles : (j + 1) * tiles
                                ]


def moments(where, f_rows, o_rows, first, last, chips, dates, tiles, slots):
    years = f_rows.shape[0]
    per_channel = chips * CORES * dates * tiles * slots
    channels = last - first
    steps = pl.cdiv(channels, BLOCK)
    in_spec = pl.BlockSpec((years, BLOCK * per_channel, LANES), lambda i, w: (0, i + first // BLOCK, 0))
    out_spec = pl.BlockSpec((FIELDS, chips, dates, BLOCK * tiles, LANES), lambda i, w: (0, 0, 0, i, 0))
    shape = jax.ShapeDtypeStruct((FIELDS, chips, dates, channels * tiles, LANES), jnp.float32)
    group = max(1, 8 // tiles)
    return pl.pallas_call(
        functools.partial(moments_kernel, chips, dates, tiles, slots),
        grid_spec=pltpu.PrefetchScalarGridSpec(
            num_scalar_prefetch=1,
            grid=(steps,),
            in_specs=[in_spec, in_spec],
            out_specs=[out_spec, out_spec],
            scratch_shapes=[pltpu.VMEM((FIELDS, group * per_channel, LANES), jnp.float32)],
        ),
        out_shape=[shape, shape],
        compiler_params=pltpu.CompilerParams(dimension_semantics=("arbitrary",)),
        cost_estimate=pl.CostEstimate(
            flops=10 * years * channels * per_channel * LANES,
            bytes_accessed=channels * per_channel * LANES * (4 * years + 4 * FIELDS // slots),
            transcendentals=0,
        ),
        name=f"moments_{first}",
    )(where, f_rows, o_rows)


def rows_of(a):
    years, _, slots, channels, grid = a.shape
    t = a.reshape(years, slots, channels, grid // LANES, LANES).transpose(0, 2, 3, 1, 4)
    return t.reshape(years, channels * (grid // LANES) * slots, LANES)


def body(predicted_anomaly, measured_anomaly, filled_calendar):
    hindcast, _, slots, channels, grid = predicted_anomaly.shape
    count = filled_calendar[0]
    n_year, n_date, n_pix = lax.axis_size("year"), lax.axis_size("date"), lax.axis_size("pix")
    chips = n_year // CORES
    tiles = grid // (LANES * n_year * n_date)
    year, date, pix = lax.axis_index("year"), lax.axis_index("date"), lax.axis_index("pix")
    core, chip = year % CORES, year // CORES
    where = jnp.stack([count, core, chip]).astype(jnp.int32)
    f_rows, o_rows = rows_of(predicted_anomaly), rows_of(measured_anomaly)
    swap = [(y, y // CORES * CORES + (y + 1) % CORES) for y in range(n_year)]

    def hop(k):
        return [(y, (y + k * CORES) % n_year) for y in range(n_year)]

    def over_dates(a):
        return lax.all_to_all(a, "date", 0, 0, tiled=True)

    edges = (0, *SPLITS, channels)
    spans = list(zip(edges[:-1], edges[1:]))
    parts = [moments(where, f_rows, o_rows, a, b, chips, n_date, tiles, slots) for a, b in spans]
    denom = hindcast * n_year * count.astype(jnp.float32)

    biases, corrected, observed = [], [], []
    for keep, send in parts:
        got = lax.ppermute(send, "year", swap)
        total = keep[:CROSS, 0] + got[:CROSS, 0]
        for k in range(1, chips):
            total = total + lax.ppermute(keep[:CROSS, k] + got[:CROSS, k], "year", hop(k))
        diff, s_o, s_ff, s_fo = total[0], total[1], total[2], total[3]
        bias = diff / denom
        biases.append(bias)
        shift = bias * s_o
        corrected.append(over_dates(jnp.stack([s_fo - shift, s_ff - 2.0 * shift - bias * diff], axis=1)))
        observed.append(jnp.swapaxes(keep[CROSS] + got[CROSS], 0, 1))
    s_oo = jnp.sum(over_dates(jnp.concatenate(observed, axis=2)), axis=0)
    own = s_oo[0]
    for k in range(1, chips):
        own = own + lax.ppermute(s_oo[k], "year", hop(k))
    sums = jnp.concatenate([jnp.sum(c, axis=0) for c in corrected], axis=1)
    s_fo, s_ff, s_oo = sums[0], jnp.maximum(sums[1], 0.0), own
    s_ee = jnp.maximum(s_ff - 2.0 * s_fo + s_oo, 0.0)
    samples = hindcast * n_year * lax.psum(count, "date").astype(jnp.float32)
    acc = (s_fo / jnp.sqrt(s_ff * s_oo + 1e-06)).reshape(channels, tiles * LANES)
    rmse = jnp.sqrt(s_ee / samples).reshape(channels, tiles * LANES)

    start = pix * grid + (year * n_date + date) * (tiles * LANES)
    global_pixel = start + jnp.arange(tiles * LANES, dtype=jnp.int32)
    lat_weight = jnp.cos((global_pixel % 181 - 90).astype(jnp.float32) * (math.pi / 180.0))
    mine = jnp.stack([jnp.sum(acc * lat_weight, axis=1), jnp.sum(rmse * lat_weight, axis=1)])
    mine = jnp.concatenate([mine, jnp.broadcast_to(jnp.sum(lat_weight), (2, 1))], axis=1)
    n_all = n_year * n_date * n_pix
    spread = lax.all_to_all(
        jnp.broadcast_to(mine[None], (n_all, *mine.shape)), ("year", "date", "pix"), 0, 0, tiled=True
    )
    sums = jnp.sum(spread, axis=0)
    scores = sums[:, :channels] / sums[:, channels:]

    bias = jnp.concatenate(
        [b.reshape(n_date, -1, tiles, LANES).transpose(1, 0, 2, 3) for b in biases], axis=0
    ).reshape(1, channels, 1, n_date * tiles * LANES)
    return (bias, acc[:, None, :], rmse[:, None, :], scores)


def solution(mesh):
    placed = (P("year", "date", None, None, "pix"), P("year", "date", None, None, "pix"), P("date"))
    return jax.shard_map(
        body,
        mesh=mesh,
        in_specs=placed,
        out_specs=(
            P("date", None, "pix", "year"),
            P(None, "pix", ("year", "date")),
            P(None, "pix", ("year", "date")),
            P(),
        ),
        check_vma=False,
    )
```

```python
import functools
import math

import jax
import jax.numpy as jnp
from jax import lax
from jax.experimental import pallas as pl
from jax.experimental.pallas import tpu as pltpu
from jax.sharding import PartitionSpec as P


LANES = 128
CORES = 2
BLOCK = 8
STEP = 32
FIELDS = 5
CROSS = 4
SPLITS = (16, 48)
EXACT = lax.Precision.HIGHEST


def place(window, own, windows):
    bits = windows.bit_length() - 1
    rank = jnp.bitwise_xor(window, own)
    return sum(((rank >> b) & 1) << (bits - 1 - b) for b in range(bits))


def window_at(position, own, windows):
    bits = windows.bit_length() - 1
    rank = sum(((position >> b) & 1) << (bits - 1 - b) for b in range(bits))
    return jnp.bitwise_xor(rank, own)


def moments_kernel(chips, dates, tiles, slots, channels, where_ref, f_ref, o_ref, keep_ref, send_ref, acc_ref):
    years = f_ref.shape[0]
    per_channel = chips * CORES * dates * tiles * slots
    group = max(1, 8 // tiles)
    count, core, chip, date = (where_ref[i] for i in range(4))
    piece = min(8, dates * tiles)
    left = jnp.minimum(BLOCK, channels - pl.program_id(0) * BLOCK)

    @pl.loop(0, (left + group - 1) // group)
    def _(g):
        for i in range(group):
            base = pl.multiple_of((g * group + i) * per_channel, per_channel)
            for sub in range(0, per_channel, STEP):
                sums = None
                for y in range(years):
                    f = f_ref[y, pl.ds(base + sub, STEP), :].astype(jnp.float32)
                    o = o_ref[y, pl.ds(base + sub, STEP), :].astype(jnp.float32)
                    terms = (f, o, f * f, f * o, o * o)
                    sums = terms if sums is None else tuple(a + b for a, b in zip(sums, terms))
                for field in range(FIELDS):
                    acc_ref[field, i * per_channel + sub : i * per_channel + sub + STEP, :] = sums[field]

        def write(used):
            for c in range(CORES):
                out_ref = (keep_ref, send_ref)[c]
                for x in range(chips):
                    block = lax.rem(chip + x, chips) * CORES + lax.rem(core + c, CORES)
                    for i in range(group):
                        row = pl.multiple_of(g * (group * tiles), group * tiles) + i * tiles
                        for p in range(0, dates * tiles, piece):
                            start = block * (dates * tiles * slots) + (i * per_channel + p * slots)
                            totals = []
                            for field in range(FIELDS):
                                total = acc_ref[field, pl.ds(start, piece, stride=slots), :]
                                for s in range(1, used):
                                    total = total + acc_ref[field, pl.ds(start + s, piece, stride=slots), :]
                                totals.append(total)
                            totals[0] = totals[0] - totals[1]
                            for j in range(piece // tiles):
                                at = place(p // tiles + j, date, dates)
                                for field in range(FIELDS):
                                    out_ref[field, at, x, pl.ds(row, tiles), :] = totals[field][
                                        j * tiles : (j + 1) * tiles
                                    ]

        for used in range(1, slots + 1):
            pl.when(count == used)(functools.partial(write, used))


def moments(where, f_rows, o_rows, first, channels, rows, chips, dates, tiles, slots):
    years = f_rows.shape[0]
    per_channel = chips * CORES * dates * tiles * slots
    in_spec = pl.BlockSpec((years, BLOCK * per_channel, LANES), lambda i, w: (0, i + first // BLOCK, 0))
    out_spec = pl.BlockSpec((FIELDS, dates, chips, BLOCK * tiles, LANES), lambda i, w: (0, 0, 0, i, 0))
    shape = jax.ShapeDtypeStruct((FIELDS, dates, chips, rows, LANES), jnp.float32)
    group = max(1, 8 // tiles)
    return pl.pallas_call(
        functools.partial(moments_kernel, chips, dates, tiles, slots, channels),
        grid_spec=pltpu.PrefetchScalarGridSpec(
            num_scalar_prefetch=1,
            grid=(pl.cdiv(channels, BLOCK),),
            in_specs=[in_spec, in_spec],
            out_specs=[out_spec, out_spec],
            scratch_shapes=[pltpu.VMEM((FIELDS, group * per_channel, LANES), jnp.float32)],
        ),
        out_shape=[shape, shape],
        compiler_params=pltpu.CompilerParams(dimension_semantics=("arbitrary",)),
        cost_estimate=pl.CostEstimate(
            flops=10 * years * channels * per_channel * LANES,
            bytes_accessed=channels * per_channel * LANES * (4 * years + 4 * FIELDS // slots),
            transcendentals=0,
        ),
        name=f"moments_{first}",
    )(where, f_rows, o_rows)


def observed_kernel(rows, where_ref, *refs):
    n = len(rows)
    keep_ref, send_ref = refs[2 * n :]
    half = pl.num_programs(0) // 2

    def fill(out_ref):
        at = 0
        for q in range(n):
            out_ref[0, :, at : at + rows[q], :] = refs[2 * q][0, 0] + refs[2 * q + 1][0, 0]
            at += rows[q]
        count = where_ref[0].astype(jnp.float32)
        for x in range(out_ref.shape[1]):
            out_ref[0, x, at - 1 : at, :] = jnp.full((1, LANES), count if x == 0 else 0.0, jnp.float32)

    pl.when(pl.program_id(0) < half)(lambda: fill(keep_ref))
    pl.when(pl.program_id(0) >= half)(lambda: fill(send_ref))


def observed(where, pairs):
    _, dates, chips, _, _ = pairs[0][0].shape
    rows = [k.shape[3] for k, _ in pairs]
    half = dates // 2
    specs, args = [], []
    for q, pair in enumerate(pairs):
        for a in pair:
            specs.append(pl.BlockSpec((1, 1, chips, rows[q], LANES), lambda p, w: (CROSS, p, 0, 0, 0)))
            args.append(a)
    shape = jax.ShapeDtypeStruct((half, chips, sum(rows), LANES), jnp.float32)
    block = (1, chips, sum(rows), LANES)
    return pl.pallas_call(
        functools.partial(observed_kernel, rows),
        grid_spec=pltpu.PrefetchScalarGridSpec(
            num_scalar_prefetch=1,
            grid=(dates,),
            in_specs=specs,
            out_specs=[
                pl.BlockSpec(block, lambda p, w: (jnp.minimum(p, half - 1), 0, 0, 0)),
                pl.BlockSpec(block, lambda p, w: (jnp.maximum(p - half, 0), 0, 0, 0)),
            ],
        ),
        out_shape=[shape, shape],
        compiler_params=pltpu.CompilerParams(dimension_semantics=("arbitrary",)),
        cost_estimate=pl.CostEstimate(
            flops=dates * chips * sum(rows) * LANES,
            bytes_accessed=12 * dates * chips * sum(rows) * LANES,
            transcendentals=0,
        ),
        name="observed",
    )(where, *args)


def corrected_kernel(scale, where_ref, keep_ref, got_ref, *refs):
    arrived, (stay_ref, leave_ref, bias_ref) = refs[:-3], refs[-3:]
    half = pl.num_programs(0) // 2
    total = keep_ref[:, 0, 0] + got_ref[:, 0, 0]
    for ref in arrived:
        total = total + ref[:, 0]
    diff, s_o, s_ff, s_fo = (total[i] for i in range(CROSS))
    bias = diff / (scale * where_ref[0].astype(jnp.float32))
    bias_ref[0] = bias
    shift = bias * s_o
    first, second = s_fo - shift, s_ff - 2.0 * shift - bias * diff

    def fill(out_ref):
        out_ref[0, 0] = first
        out_ref[0, 1] = second

    pl.when(pl.program_id(0) < half)(lambda: fill(stay_ref))
    pl.when(pl.program_id(0) >= half)(lambda: fill(leave_ref))


def corrected(where, scale, keep, got, arrived, span):
    _, dates, _, rows, _ = keep.shape
    half = dates // 2
    near = pl.BlockSpec((CROSS, 1, 1, rows, LANES), lambda p, w: (0, p, 0, 0, 0))
    far = pl.BlockSpec((CROSS, 1, rows, LANES), lambda p, w: (0, p, 0, 0))
    block = (1, 2, rows, LANES)
    shape = jax.ShapeDtypeStruct((half, 2, rows, LANES), jnp.float32)
    return pl.pallas_call(
        functools.partial(corrected_kernel, scale),
        grid_spec=pltpu.PrefetchScalarGridSpec(
            num_scalar_prefetch=1,
            grid=(dates,),
            in_specs=[near, near] + [far] * len(arrived),
            out_specs=[
                pl.BlockSpec(block, lambda p, w: (jnp.minimum(p, half - 1), 0, 0, 0)),
                pl.BlockSpec(block, lambda p, w: (jnp.maximum(p - half, 0), 0, 0, 0)),
                pl.BlockSpec((1, rows, LANES), lambda p, w: (window_at(p, w[3], dates), 0, 0)),
            ],
        ),
        out_shape=[shape, shape, jax.ShapeDtypeStruct((dates, rows, LANES), jnp.float32)],
        compiler_params=pltpu.CompilerParams(dimension_semantics=("arbitrary",)),
        cost_estimate=pl.CostEstimate(
            flops=20 * dates * rows * LANES,
            bytes_accessed=4 * dates * rows * LANES * (CROSS * (2 + len(arrived)) + 3),
            transcendentals=0,
        ),
        name=f"corrected_{span}",
    )(where, keep, got, *arrived)


def maps_kernel(scale, channels, tiles, rows, terms, weight_ref, *refs):
    refs = list(refs)
    parts = [[refs.pop(0) for _ in range(terms)] for _ in rows]
    oo_refs = [refs.pop(0) for _ in range(len(refs) - 3)]
    acc_ref, rmse_ref, part_ref = refs
    s_oo = sum(r[0, 0] for r in oo_refs[1:terms]) + oo_refs[0][0, 0]
    for r in oo_refs[terms:]:
        s_oo = s_oo + r[...]
    n = channels * tiles
    samples = scale * s_oo[s_oo.shape[0] - 1 :, 0:1]
    weight = weight_ref[...]
    lines = []
    for kind in range(2):
        lines.append([])
    at = 0
    for q, part in enumerate(parts):
        s_fo, s_ff = (sum(r[0, i] for r in part[1:]) + part[0][0, i] for i in range(2))
        oo = s_oo[at : at + rows[q]]
        s_ff = jnp.maximum(s_ff, 0.0)
        s_ee = jnp.maximum(s_ff - 2.0 * s_fo + oo, 0.0)
        acc = s_fo / jnp.sqrt(s_ff * oo + 1e-06)
        rmse = jnp.sqrt(s_ee / samples)
        take = min(rows[q], n - at)
        acc_ref[at : at + take, :] = acc[:take]
        rmse_ref[at : at + take, :] = rmse[:take]
        inside = lax.broadcasted_iota(jnp.int32, (rows[q], LANES), 0) < n - at
        tall = jnp.concatenate([weight] * (rows[q] // 8), axis=0)
        pick = lax.broadcasted_iota(jnp.int32, (rows[q], LANES), 0) + at
        pick = (pick // tiles == lax.broadcasted_iota(jnp.int32, (rows[q], LANES), 1)).astype(jnp.float32)
        for kind, value in enumerate((acc, rmse)):
            weighted = jnp.where(inside, value * tall, 0.0)
            line = lax.dot_general(
                jnp.ones((8, LANES), jnp.float32),
                weighted,
                (((1,), (1,)), ((), ())),
                precision=EXACT,
                preferred_element_type=jnp.float32,
            )
            lines[kind].append(
                lax.dot_general(
                    line, pick, (((1,), (0,)), ((), ())), precision=EXACT, preferred_element_type=jnp.float32
                )
            )
        at += rows[q]
    for kind in range(2):
        part_ref[:, kind, :] = jnp.broadcast_to(sum(lines[kind])[0:1], (part_ref.shape[0], LANES))


def maps(scale, channels, tiles, weight, parts, oo_parts, oo_arrived, copies):
    rows = [p[0].shape[2] for p in parts]
    specs = [pl.BlockSpec((8, LANES), lambda i: (0, 0))]
    args = [weight]
    for part in parts:
        for a in part:
            specs.append(pl.BlockSpec((1, 2, a.shape[2], LANES), lambda i: (0, 0, 0, 0)))
            args.append(a)
    for a in oo_parts:
        specs.append(pl.BlockSpec((1, 1, a.shape[2], LANES), lambda i: (0, 0, 0, 0)))
        args.append(a)
    for a in oo_arrived:
        specs.append(pl.BlockSpec(a.shape, lambda i: (0, 0)))
        args.append(a)
    n = channels * tiles
    flat = jax.ShapeDtypeStruct((n, LANES), jnp.float32)
    return pl.pallas_call(
        functools.partial(maps_kernel, scale, channels, tiles, rows, len(parts[0])),
        grid=(1,),
        in_specs=specs,
        out_specs=[
            pl.BlockSpec((n, LANES), lambda i: (0, 0)),
            pl.BlockSpec((n, LANES), lambda i: (0, 0)),
            pl.BlockSpec((copies, 2, LANES), lambda i: (0, 0, 0)),
        ],
        out_shape=[flat, flat, jax.ShapeDtypeStruct((copies, 2, LANES), jnp.float32)],
        cost_estimate=pl.CostEstimate(flops=40 * n * LANES, bytes_accessed=40 * n * LANES, transcendentals=0),
        name="maps",
    )(*args)


def rows_of(a):
    years, _, slots, channels, grid = a.shape
    t = a.reshape(years, slots, channels, grid // LANES, LANES).transpose(0, 2, 3, 1, 4)
    return t.reshape(years, channels * (grid // LANES) * slots, LANES)


def latitude_weight(pixel):
    return jnp.cos((pixel % 181 - 90).astype(jnp.float32) * (math.pi / 180.0))


def body(predicted_anomaly, measured_anomaly, filled_calendar):
    hindcast, _, slots, channels, grid = predicted_anomaly.shape
    n_year, n_date, n_pix = lax.axis_size("year"), lax.axis_size("date"), lax.axis_size("pix")
    chips = n_year // CORES
    tiles = grid // (LANES * n_year * n_date)
    year, date, pix = lax.axis_index("year"), lax.axis_index("date"), lax.axis_index("pix")
    where = jnp.stack([filled_calendar[0], year % CORES, year // CORES, date]).astype(jnp.int32)
    f_rows, o_rows = rows_of(predicted_anomaly), rows_of(measured_anomaly)
    swap = [(y, y // CORES * CORES + (y + 1) % CORES) for y in range(n_year)]
    scale = float(hindcast * n_year)

    def hop(a, k):
        return lax.ppermute(a, "year", [(y, (y + k * CORES) % n_year) for y in range(n_year)])

    def halve(stay, leave):
        got = [lax.ppermute(leave, "date", [(d, d ^ 1) for d in range(n_date)])]
        k, half = 2, n_date // 4
        while half:
            leave = stay[half : 2 * half] + sum(g[half : 2 * half] for g in got)
            got.append(lax.ppermute(leave, "date", [(d, d ^ k) for d in range(n_date)]))
            k, half = 2 * k, half // 2
        return [stay, *got]

    edges = (0, *SPLITS, channels)
    pairs, biases, parts = [], [], []
    for first, last in zip(edges[:-1], edges[1:]):
        size = last - first
        rows = (size * tiles + (last == channels) + 7) // 8 * 8
        keep, send = moments(where, f_rows, o_rows, first, size, rows, chips, n_date, tiles, slots)
        got = lax.ppermute(send, "year", swap)
        pairs.append((keep, got))
    for q, (keep, got) in enumerate(pairs):
        arrived = [hop(keep[:CROSS, :, k] + got[:CROSS, :, k], k) for k in range(1, chips)]
        stay, leave, bias = corrected(where, scale, keep, got, arrived, q)
        biases.append(bias)
        parts.append(halve(stay, leave))
    oo_parts = halve(*observed(where, pairs))
    oo_arrived = [hop(sum(p[0, k] for p in oo_parts), k) for k in range(1, chips)]

    start = pix * grid + (year * n_date + date) * (tiles * LANES)
    row = jnp.arange(8, dtype=jnp.int32)[:, None] % tiles
    weight = latitude_weight(start + row * LANES + jnp.arange(LANES, dtype=jnp.int32)[None, :])
    weight_total = jnp.sum(latitude_weight(jnp.arange(n_pix * grid, dtype=jnp.int32)))
    acc, rmse, part = maps(
        scale, channels, tiles, weight, parts, oo_parts, oo_arrived, n_year * n_date * n_pix
    )
    spread = lax.all_to_all(part, ("year", "date", "pix"), 0, 0, tiled=True)
    scores = jnp.sum(spread, axis=0)[:, :channels] / weight_total

    cut = [b[:, : (last - first) * tiles] for b, first, last in zip(biases, edges[:-1], edges[1:])]
    bias = jnp.concatenate(cut, axis=1).reshape(n_date, channels, tiles, LANES).transpose(1, 0, 2, 3)
    flat = (channels, 1, tiles * LANES)
    return (bias.reshape(1, channels, 1, -1), acc.reshape(flat), rmse.reshape(flat), scores)


def solution(mesh):
    placed = (P("year", "date", None, None, "pix"), P("year", "date", None, None, "pix"), P("date"))
    return jax.shard_map(
        body,
        mesh=mesh,
        in_specs=placed,
        out_specs=(
            P("date", None, "pix", "year"),
            P(None, "pix", ("year", "date")),
            P(None, "pix", ("year", "date")),
            P(),
        ),
        check_vma=False,
    )
```

```python
import functools
import math

import jax
import jax.numpy as jnp
from jax import lax
from jax.experimental import pallas as pl
from jax.experimental.pallas import tpu as pltpu
from jax.sharding import PartitionSpec as P


LANES = 128
CORES = 2
BLOCK = 8
STEP = 32
FIELDS = 5
CROSS = 4
SPLITS = (16, 48)
EXACT = lax.Precision.HIGHEST
GRANT = 12 << 20


def place(window, own, windows):
    bits = windows.bit_length() - 1
    rank = jnp.bitwise_xor(window, own)
    return sum(((rank >> b) & 1) << (bits - 1 - b) for b in range(bits))


def window_at(position, own, windows):
    bits = windows.bit_length() - 1
    rank = sum(((position >> b) & 1) << (bits - 1 - b) for b in range(bits))
    return jnp.bitwise_xor(rank, own)


def moments_kernel(chips, dates, tiles, slots, channels, where_ref, f_ref, o_ref, *refs):
    keep_ref, send_ref, acc_ref = refs[-3:]
    years = f_ref.shape[0]
    per_channel = chips * CORES * dates * tiles * slots
    group = max(1, 8 // tiles)
    step = pl.program_id(0) * BLOCK
    count, core, chip, date = (where_ref[i] for i in range(4))
    piece = min(8, dates * tiles)
    left = jnp.minimum(BLOCK, channels - step)

    @pl.loop(0, (left + group - 1) // group)
    def _(g):
        @pl.loop(0, group)
        def _(i):
            base = pl.multiple_of((g * group + i) * per_channel, per_channel)
            into = pl.multiple_of(i * per_channel, per_channel)
            for sub in range(0, per_channel, STEP):
                sums = None
                for y in range(years):
                    f = f_ref[y, pl.ds(base + sub, STEP), :].astype(jnp.float32)
                    o = o_ref[y, pl.ds(base + sub, STEP), :].astype(jnp.float32)
                    terms = (f, o, f * f, f * o, o * o)
                    sums = terms if sums is None else tuple(a + b for a, b in zip(sums, terms))
                for field in range(FIELDS):
                    acc_ref[field, pl.ds(into + sub, STEP), :] = sums[field]

        def write(used):
            for c in range(CORES):
                out_ref = (keep_ref, send_ref)[c]

                @pl.loop(0, chips)
                def _(x):
                    block = lax.rem(chip + x, chips) * CORES + lax.rem(core + c, CORES)
                    for i in range(group):
                        row = pl.multiple_of(step * tiles + g * (group * tiles), group * tiles) + i * tiles
                        for p in range(0, dates * tiles, piece):
                            start = block * (dates * tiles * slots) + (i * per_channel + p * slots)
                            totals = []
                            for field in range(FIELDS):
                                total = acc_ref[field, pl.ds(start, piece, stride=slots), :]
                                for s in range(1, used):
                                    total = total + acc_ref[field, pl.ds(start + s, piece, stride=slots), :]
                                totals.append(total)
                            totals[0] = totals[0] - totals[1]
                            for j in range(piece // tiles):
                                at = place(p // tiles + j, date, dates)
                                for field in range(FIELDS):
                                    out_ref[field, at, x, pl.ds(row, tiles), :] = totals[field][
                                        j * tiles : (j + 1) * tiles
                                    ]

        for used in range(1, slots + 1):
            pl.when(count == used)(functools.partial(write, used))


def moments(where, f_rows, o_rows, after, first, channels, rows, chips, dates, tiles, slots):
    years = f_rows.shape[0]
    per_channel = chips * CORES * dates * tiles * slots
    in_spec = pl.BlockSpec((years, BLOCK * per_channel, LANES), lambda i, w: (0, i + first // BLOCK, 0))
    out_spec = pl.BlockSpec(memory_space=pltpu.VMEM)
    shape = pltpu.VMEM((FIELDS, dates, chips, rows, LANES), jnp.float32)
    group = max(1, 8 // tiles)
    return pl.pallas_call(
        functools.partial(moments_kernel, chips, dates, tiles, slots, channels),
        grid_spec=pltpu.PrefetchScalarGridSpec(
            num_scalar_prefetch=1,
            grid=(pl.cdiv(channels, BLOCK),),
            in_specs=[in_spec, in_spec] + [pl.BlockSpec(memory_space=pl.ANY)] * len(after),
            out_specs=[out_spec, out_spec],
            scratch_shapes=[pltpu.VMEM((FIELDS, group * per_channel, LANES), jnp.float32)],
        ),
        out_shape=[shape, shape],
        compiler_params=pltpu.CompilerParams(dimension_semantics=("arbitrary",), vmem_limit_bytes=GRANT),
        cost_estimate=pl.CostEstimate(
            flops=10 * years * channels * per_channel * LANES,
            bytes_accessed=channels * per_channel * LANES * (4 * years + 4 * FIELDS // slots),
            transcendentals=0,
        ),
    )(where, *(pltpu.with_memory_space_constraint(a, pltpu.HBM) for a in (f_rows, o_rows)), *after)


def in_vmem(n):
    return [pl.BlockSpec(memory_space=pltpu.VMEM)] * n


def in_smem():
    return [pl.BlockSpec(memory_space=pltpu.SMEM)]


def held(arrays):
    return [pltpu.with_memory_space_constraint(a, pltpu.VMEM) for a in arrays]


def observed_kernel(rows, where_ref, *refs):
    n = len(rows)
    keep_ref, send_ref = refs[2 * n :]
    half, chips = keep_ref.shape[:2]
    count = where_ref[0].astype(jnp.float32)
    for p in range(2 * half):
        out_ref = keep_ref if p < half else send_ref
        at = 0
        for q in range(n):
            out_ref[p % half, :, at : at + rows[q], :] = refs[2 * q][CROSS, p] + refs[2 * q + 1][CROSS, p]
            at += rows[q]
        for x in range(chips):
            out_ref[p % half, x, at - 1 : at, :] = jnp.full((1, LANES), count if x == 0 else 0.0, jnp.float32)


def observed(where, pairs):
    _, dates, chips, _, _ = pairs[0][0].shape
    rows = [k.shape[3] for k, _ in pairs]
    args = held([a for pair in pairs for a in pair])
    shape = pltpu.VMEM((dates // 2, chips, sum(rows), LANES), jnp.float32)
    return pl.pallas_call(
        functools.partial(observed_kernel, rows),
        in_specs=in_smem() + in_vmem(len(args)),
        out_specs=in_vmem(2),
        out_shape=[shape, shape],
        compiler_params=pltpu.CompilerParams(vmem_limit_bytes=GRANT),
        cost_estimate=pl.CostEstimate(
            flops=dates * chips * sum(rows) * LANES,
            bytes_accessed=12 * dates * chips * sum(rows) * LANES,
            transcendentals=0,
        ),
        name="observed",
    )(where, *args)


def corrected_kernel(scale, where_ref, keep_ref, got_ref, *refs):
    arrived, (stay_ref, leave_ref, bias_ref) = refs[:-3], refs[-3:]
    half = stay_ref.shape[0]
    samples = scale * where_ref[0].astype(jnp.float32)
    for p in range(2 * half):
        out_ref = stay_ref if p < half else leave_ref
        total = keep_ref[:CROSS, p, 0] + got_ref[:CROSS, p, 0]
        for ref in arrived:
            total = total + ref[:, p]
        diff, s_o, s_ff, s_fo = (total[i] for i in range(CROSS))
        bias = diff / samples
        bias_ref[window_at(jnp.int32(p), where_ref[3], 2 * half)] = bias
        shift = bias * s_o
        out_ref[p % half, 0] = s_fo - shift
        out_ref[p % half, 1] = s_ff - 2.0 * shift - bias * diff


def corrected(where, scale, keep, got, arrived):
    _, dates, _, rows, _ = keep.shape
    args = held([keep, got, *arrived])
    shape = pltpu.VMEM((dates // 2, 2, rows, LANES), jnp.float32)
    return pl.pallas_call(
        functools.partial(corrected_kernel, scale),
        in_specs=in_smem() + in_vmem(len(args)),
        out_specs=in_vmem(3),
        out_shape=[shape, shape, pltpu.VMEM((dates, rows, LANES), jnp.float32)],
        compiler_params=pltpu.CompilerParams(vmem_limit_bytes=GRANT),
        cost_estimate=pl.CostEstimate(
            flops=20 * dates * rows * LANES,
            bytes_accessed=4 * dates * rows * LANES * (CROSS * (2 + len(arrived)) + 3),
            transcendentals=0,
        ),
    )(where, *args)


def maps_kernel(scale, channels, tiles, rows, terms, weight_ref, *refs):
    refs = list(refs)
    parts = [[refs.pop(0) for _ in range(terms)] for _ in rows]
    oo_refs = [refs.pop(0) for _ in range(len(refs) - 3)]
    acc_ref, rmse_ref, part_ref = refs
    s_oo = sum(r[0, 0] for r in oo_refs[1:terms]) + oo_refs[0][0, 0]
    for r in oo_refs[terms:]:
        s_oo = s_oo + r[...]
    n = channels * tiles
    samples = scale * s_oo[s_oo.shape[0] - 1 :, 0:1]
    weight = weight_ref[...]
    lines = []
    for _ in range(2):
        lines.append([])
    at = 0
    for q, part in enumerate(parts):
        s_fo, s_ff = (sum(r[0, i] for r in part[1:]) + part[0][0, i] for i in range(2))
        oo = s_oo[at : at + rows[q]]
        s_ff = jnp.maximum(s_ff, 0.0)
        s_ee = jnp.maximum(s_ff - 2.0 * s_fo + oo, 0.0)
        acc = s_fo / jnp.sqrt(s_ff * oo + 1e-06)
        rmse = jnp.sqrt(s_ee / samples)
        take = min(rows[q], n - at)
        acc_ref[at : at + take, :] = acc[:take]
        rmse_ref[at : at + take, :] = rmse[:take]
        inside = lax.broadcasted_iota(jnp.int32, (rows[q], LANES), 0) < n - at
        tall = jnp.concatenate([weight] * (rows[q] // 8), axis=0)
        pick = lax.broadcasted_iota(jnp.int32, (rows[q], LANES), 0) + at
        pick = (pick // tiles == lax.broadcasted_iota(jnp.int32, (rows[q], LANES), 1)).astype(jnp.float32)
        for kind, value in enumerate((acc, rmse)):
            weighted = jnp.where(inside, value * tall, 0.0)
            line = lax.dot_general(
                jnp.ones((8, LANES), jnp.float32),
                weighted,
                (((1,), (1,)), ((), ())),
                precision=EXACT,
                preferred_element_type=jnp.float32,
            )
            lines[kind].append(
                lax.dot_general(
                    line, pick, (((1,), (0,)), ((), ())), precision=EXACT, preferred_element_type=jnp.float32
                )
            )
        at += rows[q]
    for kind in range(2):
        part_ref[:, kind, :] = jnp.broadcast_to(sum(lines[kind])[0:1], (part_ref.shape[0], LANES))


def maps(scale, channels, tiles, weight, parts, oo_parts, oo_arrived, copies):
    rows = [p[0].shape[2] for p in parts]
    args = held([weight, *(a for part in parts for a in part), *oo_parts, *oo_arrived])
    n = channels * tiles
    flat = pltpu.VMEM((n, LANES), jnp.float32)
    return pl.pallas_call(
        functools.partial(maps_kernel, scale, channels, tiles, rows, len(parts[0])),
        in_specs=in_vmem(len(args)),
        out_specs=in_vmem(3),
        out_shape=[flat, flat, pltpu.VMEM((copies, 2, LANES), jnp.float32)],
        compiler_params=pltpu.CompilerParams(vmem_limit_bytes=GRANT),
        cost_estimate=pl.CostEstimate(flops=40 * n * LANES, bytes_accessed=40 * n * LANES, transcendentals=0),
        name="maps",
    )(*args)


def rows_of(a):
    years, _, slots, channels, grid = a.shape
    t = a.reshape(years, slots, channels, grid // LANES, LANES).transpose(0, 2, 3, 1, 4)
    return t.reshape(years, channels * (grid // LANES) * slots, LANES)


def latitude_weight(pixel):
    return jnp.cos((pixel % 181 - 90).astype(jnp.float32) * (math.pi / 180.0))


def step(predicted_anomaly, measured_anomaly, filled_calendar):
    hindcast, _, slots, channels, grid = predicted_anomaly.shape
    n_year, n_date, n_pix = lax.axis_size("year"), lax.axis_size("date"), lax.axis_size("pix")
    chips = n_year // CORES
    tiles = grid // (LANES * n_year * n_date)
    year, date, pix = lax.axis_index("year"), lax.axis_index("date"), lax.axis_index("pix")
    where = jnp.stack([filled_calendar[0], year % CORES, year // CORES, date]).astype(jnp.int32)
    f_rows, o_rows = rows_of(predicted_anomaly), rows_of(measured_anomaly)
    swap = [(y, y // CORES * CORES + (y + 1) % CORES) for y in range(n_year)]
    scale = float(hindcast * n_year)

    def hop(a, k):
        return lax.ppermute(a, "year", [(y, (y + k * CORES) % n_year) for y in range(n_year)])

    def halve(stay, leave):
        got = [lax.ppermute(leave, "date", [(d, d ^ 1) for d in range(n_date)])]
        k, half = 2, n_date // 4
        while half:
            leave = stay[half : 2 * half] + sum(g[half : 2 * half] for g in got)
            got.append(lax.ppermute(leave, "date", [(d, d ^ k) for d in range(n_date)]))
            k, half = 2 * k, half // 2
        return [stay, *got]

    edges = (0, *SPLITS, channels)
    pairs, biases, parts, leaving = [], [], [], []
    after = []
    for first, last in zip(edges[:-1], edges[1:]):
        size = last - first
        rows = (size * tiles + (last == channels) + 7) // 8 * 8
        keep, send = moments(where, f_rows, o_rows, after, first, size, rows, chips, n_date, tiles, slots)
        got = lax.ppermute(send, "year", swap)
        pairs.append((keep, got))
        leaving.append([keep[:CROSS, :, k] + got[:CROSS, :, k] for k in range(1, chips)])
        after = leaving[-1]
    for q, (keep, got) in enumerate(pairs):
        arrived = [hop(a, k + 1) for k, a in enumerate(leaving[q])]
        stay, leave, bias = corrected(where, scale, keep, got, arrived)
        biases.append(bias)
        parts.append(halve(stay, leave))
    oo_parts = halve(*observed(where, pairs))
    oo_arrived = [hop(sum(p[0, k] for p in oo_parts), k) for k in range(1, chips)]

    start = pix * grid + (year * n_date + date) * (tiles * LANES)
    row = jnp.arange(8, dtype=jnp.int32)[:, None] % tiles
    weight = latitude_weight(start + row * LANES + jnp.arange(LANES, dtype=jnp.int32)[None, :])
    weight_total = jnp.sum(latitude_weight(jnp.arange(n_pix * grid, dtype=jnp.int32)))
    acc, rmse, part = maps(
        scale, channels, tiles, weight, parts, oo_parts, oo_arrived, n_year * n_date * n_pix
    )
    spread = lax.all_to_all(part, ("year", "date", "pix"), 0, 0, tiled=True)
    scores = jnp.sum(spread, axis=0)[:, :channels] / weight_total

    cut = [b[:, : (last - first) * tiles] for b, first, last in zip(biases, edges[:-1], edges[1:])]
    bias = jnp.concatenate(cut, axis=1).reshape(n_date, channels, tiles, LANES).transpose(1, 0, 2, 3)
    flat = (channels, 1, tiles * LANES)
    return (bias.reshape(1, channels, 1, -1), acc.reshape(flat), rmse.reshape(flat), scores)


def solution(mesh):
    placed = (P("year", "date", None, None, "pix"), P("year", "date", None, None, "pix"), P("date"))
    return jax.shard_map(
        step,
        mesh=mesh,
        in_specs=placed,
        out_specs=(
            P("date", None, "pix", "year"),
            P(None, "pix", ("year", "date")),
            P(None, "pix", ("year", "date")),
            P(),
        ),
        check_vma=False,
    )
```

```python
import functools
import math

import jax
import jax.numpy as jnp
from jax import lax
from jax.experimental import pallas as pl
from jax.experimental.pallas import tpu as pltpu
from jax.sharding import PartitionSpec as P


LANES = 128
CORES = 2
BLOCK = 8
STEP = 32
FIELDS = 5
SPLITS = (16, 48, 72)
KINDS = (4, 4, 4, 5)
EXACT = lax.Precision.HIGHEST
GRANT = 6 << 20


def place(window, own, windows):
    bits = windows.bit_length() - 1
    rank = jnp.bitwise_xor(window, own)
    return sum(((rank >> b) & 1) << (bits - 1 - b) for b in range(bits))


def window_at(position, own, windows):
    bits = windows.bit_length() - 1
    rank = sum(((position >> b) & 1) << (bits - 1 - b) for b in range(bits))
    return jnp.bitwise_xor(rank, own)


def moments_kernel(chips, dates, tiles, slots, channels, cross, where_ref, f_ref, o_ref, *refs):
    outs, acc_ref = refs[-5:-1], refs[-1]
    years = f_ref.shape[0]
    per_channel = chips * CORES * dates * tiles * slots
    group = max(1, 8 // tiles)
    step = pl.program_id(0) * BLOCK
    count, date, year = where_ref[0], lax.axis_index("date"), lax.axis_index("year")
    core, chip = lax.rem(year, CORES), year // CORES
    piece = min(8, dates * tiles)
    left = jnp.minimum(BLOCK, channels - step)

    @pl.loop(0, (left + group - 1) // group)
    def _(g):
        @pl.loop(0, group)
        def _(i):
            base = pl.multiple_of((g * group + i) * per_channel, per_channel)
            into = pl.multiple_of(i * per_channel, per_channel)
            for sub in range(0, per_channel, STEP):
                sums = None
                for y in range(years):
                    f = f_ref[y, pl.ds(base + sub, STEP), :].astype(jnp.float32)
                    o = o_ref[y, pl.ds(base + sub, STEP), :].astype(jnp.float32)
                    terms = (f, o, f * o, f * f, o * o)
                    sums = terms if sums is None else tuple(a + b for a, b in zip(sums, terms))
                for field in range(FIELDS):
                    acc_ref[field, pl.ds(into + sub, STEP), :] = sums[field]

        def write(used, c, x):
            away_ref, rest_ref = outs[2 * c : 2 * c + 2]
            block = lax.rem(chip + x, chips) * CORES + lax.rem(core + c, CORES)
            for i in range(group):
                row = pl.multiple_of(step * tiles + g * (group * tiles), group * tiles) + i * tiles
                for p in range(0, dates * tiles, piece):
                    start = block * (dates * tiles * slots) + (i * per_channel + p * slots)
                    totals = []
                    for field in range(FIELDS):
                        total = acc_ref[field, pl.ds(start, piece, stride=slots), :]
                        for s in range(1, used):
                            total = total + acc_ref[field, pl.ds(start + s, piece, stride=slots), :]
                        totals.append(total)
                    totals[0] = totals[0] - totals[1]
                    for j in range(piece // tiles):
                        at = place(p // tiles + j, date, dates)
                        for field in range(FIELDS):
                            value = totals[field][j * tiles : (j + 1) * tiles]
                            if field >= cross:
                                rest_ref[cross + (field - cross) * chips + x, at, pl.ds(row, tiles), :] = value
                            elif isinstance(x, int):
                                rest_ref[field, at, pl.ds(row, tiles), :] = value
                            else:
                                away_ref[field, at, x - 1, pl.ds(row, tiles), :] = value

        def write_all(used):
            for c in range(CORES):
                write(used, c, 0)
                pl.loop(1, chips)(functools.partial(write, used, c))

        for used in range(1, slots + 1):
            pl.when(count == used)(functools.partial(write_all, used))


def moments(where, f_rows, o_rows, after, first, channels, rows, cross, chips, dates, tiles, slots):
    years = f_rows.shape[0]
    per_channel = chips * CORES * dates * tiles * slots
    in_spec = pl.BlockSpec((years, BLOCK * per_channel, LANES), lambda i, w: (0, i + first // BLOCK, 0))
    away = pltpu.VMEM((cross, dates, chips - 1, rows, LANES), jnp.float32)
    rest = pltpu.VMEM((cross + (FIELDS - cross) * chips, dates, rows, LANES), jnp.float32)
    group = max(1, 8 // tiles)
    window = years * BLOCK * per_channel * LANES * f_rows.dtype.itemsize
    need = 4 * window + 4 * FIELDS * group * per_channel * LANES
    return pl.pallas_call(
        functools.partial(moments_kernel, chips, dates, tiles, slots, channels, cross),
        grid_spec=pltpu.PrefetchScalarGridSpec(
            num_scalar_prefetch=1,
            grid=(pl.cdiv(channels, BLOCK),),
            in_specs=[in_spec, in_spec] + [pl.BlockSpec(memory_space=pl.ANY)] * len(after),
            out_specs=in_vmem(4),
            scratch_shapes=[pltpu.VMEM((FIELDS, group * per_channel, LANES), jnp.float32)],
        ),
        out_shape=[away, rest, away, rest],
        compiler_params=pltpu.CompilerParams(dimension_semantics=("arbitrary",), vmem_limit_bytes=need + (2 << 20)),
        cost_estimate=pl.CostEstimate(
            flops=10 * years * channels * per_channel * LANES,
            bytes_accessed=channels * per_channel * LANES * (4 * years + 4 * FIELDS // slots),
            transcendentals=0,
        ),
    )(where, *(pltpu.with_memory_space_constraint(a, pltpu.HBM) for a in (f_rows, o_rows)), *after)


def in_vmem(n):
    return [pl.BlockSpec(memory_space=pltpu.VMEM)] * n


def in_smem():
    return [pl.BlockSpec(memory_space=pltpu.SMEM)]


def held(arrays):
    return [pltpu.with_memory_space_constraint(a, pltpu.VMEM) for a in arrays]


def observed_kernel(segments, kinds, where_ref, *refs):
    pairs, (keep_ref, send_ref) = refs[:-2], refs[-2:]
    half, chips, total, _ = keep_ref.shape
    count = where_ref[0].astype(jnp.float32)
    for p in range(2 * half):
        out_ref = keep_ref if p < half else send_ref
        for x in range(chips):
            for (q, field), (at, n) in segments.items():
                plane = kinds[q] + (field - kinds[q]) * chips + x
                out_ref[p % half, x, at : at + n, :] = pairs[2 * q][plane, p] + pairs[2 * q + 1][plane, p]
            used = jnp.full((8, LANES), count if x == 0 else 0.0, jnp.float32)
            out_ref[p % half, x, total - 8 : total, :] = used


def observed(where, chips, segments, kinds, pairs):
    dates = pairs[0][0].shape[1]
    total = sum(n for _, n in segments.values()) + 8
    args = held([a for pair in pairs for a in pair])
    shape = pltpu.VMEM((dates // 2, chips, total, LANES), jnp.float32)
    return pl.pallas_call(
        functools.partial(observed_kernel, segments, kinds),
        in_specs=in_smem() + in_vmem(len(args)),
        out_specs=in_vmem(2),
        out_shape=[shape, shape],
        compiler_params=pltpu.CompilerParams(vmem_limit_bytes=GRANT),
        cost_estimate=pl.CostEstimate(
            flops=dates * chips * total * LANES,
            bytes_accessed=12 * dates * chips * total * LANES,
            transcendentals=0,
        ),
        name="observed",
    )(where, *args)


def corrected_kernel(scale, cross, where_ref, keep_ref, got_ref, *refs):
    arrived, (stay_ref, leave_ref, bias_ref) = refs[:-3], refs[-3:]
    half = stay_ref.shape[0]
    samples = scale * where_ref[0].astype(jnp.float32)
    date = lax.axis_index("date")
    for p in range(2 * half):
        out_ref = stay_ref if p < half else leave_ref
        total = keep_ref[:cross, p] + got_ref[:cross, p]
        for ref in arrived:
            total = total + ref[:, p]
        diff, s_o, s_fo = (total[i] for i in range(3))
        bias = diff / samples
        bias_ref[window_at(jnp.int32(p), date, 2 * half)] = bias
        shift = bias * s_o
        out_ref[p % half, 0] = s_fo - shift
        change = 2.0 * shift + bias * diff
        out_ref[p % half, 1] = total[3] - change if cross > 3 else -change
        if cross == FIELDS:
            out_ref[p % half, 2] = total[4]


def corrected(where, scale, cross, keep, got, arrived):
    _, dates, rows, _ = keep.shape
    args = held([keep, got, *arrived])
    shape = pltpu.VMEM((dates // 2, 2 + (cross == FIELDS), rows, LANES), jnp.float32)
    return pl.pallas_call(
        functools.partial(corrected_kernel, scale, cross),
        in_specs=in_smem() + in_vmem(len(args)),
        out_specs=in_vmem(3),
        out_shape=[shape, shape, pltpu.VMEM((dates, rows, LANES), jnp.float32)],
        compiler_params=pltpu.CompilerParams(vmem_limit_bytes=GRANT),
        cost_estimate=pl.CostEstimate(
            flops=20 * dates * rows * LANES,
            bytes_accessed=4 * dates * rows * LANES * (cross * (2 + len(arrived)) + 3),
            transcendentals=0,
        ),
    )(where, *args)


def span_maps(parts, ff, oo, samples, weight, pick_ref, at, limit, acc_ref, rmse_ref, base):
    s_fo, s_ff = (sum(r[0, i] for r in parts[1:]) + parts[0][0, i] for i in range(2))
    if oo is None:
        oo = sum(r[0, 2] for r in parts[1:]) + parts[0][0, 2]
    if ff is not None:
        s_ff = s_ff + ff
    rows = s_fo.shape[0]
    s_ff = jnp.maximum(s_ff, 0.0)
    s_ee = jnp.maximum(s_ff - 2.0 * s_fo + oo, 0.0)
    acc = s_fo / jnp.sqrt(s_ff * oo + 1e-06)
    rmse = jnp.sqrt(s_ee / samples)
    take = min(rows, limit - at)
    acc_ref[at - base : at - base + take, :] = acc[:take]
    rmse_ref[at - base : at - base + take, :] = rmse[:take]
    tall = jnp.concatenate([weight] * (rows // 8), axis=0)
    weighted = jnp.concatenate([acc * tall, rmse * tall], axis=1)
    if take < rows:
        weighted = jnp.where(lax.broadcasted_iota(jnp.int32, weighted.shape, 0) < take, weighted, 0.0)
    by_channel = lax.dot_general(
        weighted,
        pick_ref[at : at + rows, :],
        (((0,), (0,)), ((), ())),
        precision=EXACT,
        preferred_element_type=jnp.float32,
    )
    lines = [jnp.sum(by_channel[k * LANES : (k + 1) * LANES], axis=0, keepdims=True) for k in range(2)]
    return lines


def early_kernel(scale, rows, segments, depth, weight_ref, pick_ref, *refs):
    acc_ref, rmse_ref, sums_ref = refs[-3:]
    n = len(rows)
    z_refs, x_refs = refs[n * depth : (n + 1) * depth], refs[(n + 1) * depth : -3]

    def gathered(at, size):
        value = sum(r[0, 0, at : at + size, :] for r in z_refs[1:]) + z_refs[0][0, 0, at : at + size, :]
        for r in x_refs:
            value = value + r[at : at + size, :]
        return value

    samples = scale * gathered(z_refs[0].shape[2] - 8, 8)[0:1, :]
    at, lines = 0, None
    for q in range(n):
        parts = refs[q * depth : (q + 1) * depth]
        ff, oo = (gathered(*segments[(q, f)]) if (q, f) in segments else None for f in (3, 4))
        new = span_maps(parts, ff, oo, samples, weight_ref[0:8, :], pick_ref, at, sum(rows), acc_ref, rmse_ref, 0)
        lines = new if lines is None else [a + b for a, b in zip(lines, new)]
        at += rows[q]
    sums_ref[0:1, :] = lines[0]
    sums_ref[1:2, :] = lines[1]
    sums_ref[2:3, :] = samples


def last_kernel(at, limit, weight_ref, pick_ref, sums_ref, *refs):
    acc_ref, rmse_ref, part_ref = refs[-3:]
    samples = sums_ref[2:3, :]
    lines = span_maps(refs[:-3], None, None, samples, weight_ref[0:8, :], pick_ref, at, limit, acc_ref, rmse_ref, at)
    for kind in range(2):
        line = (lines[kind] + sums_ref[kind : kind + 1, :]) / weight_ref[8:9, :]
        part_ref[:, kind, :] = jnp.broadcast_to(line, (part_ref.shape[0], LANES))


def maps_call(kernel, n, third, args):
    args = held(args)
    flat = pltpu.VMEM((n, LANES), jnp.float32)
    return pl.pallas_call(
        kernel,
        in_specs=in_vmem(len(args)),
        out_specs=in_vmem(3),
        out_shape=[flat, flat, pltpu.VMEM(third, jnp.float32)],
        compiler_params=pltpu.CompilerParams(vmem_limit_bytes=GRANT),
        cost_estimate=pl.CostEstimate(flops=40 * n * LANES, bytes_accessed=40 * n * LANES, transcendentals=0),
    )(*args)


def scores_kernel(spread_ref, out_ref):
    sums = spread_ref[0]
    for i in range(1, spread_ref.shape[0]):
        sums = sums + spread_ref[i]
    out_ref[...] = sums[:, : out_ref.shape[1]]


def scores_of(spread, channels):
    return pl.pallas_call(
        scores_kernel,
        in_specs=in_vmem(1),
        out_specs=pl.BlockSpec(memory_space=pltpu.VMEM),
        out_shape=jax.ShapeDtypeStruct((2, channels), jnp.float32),
        compiler_params=pltpu.CompilerParams(vmem_limit_bytes=GRANT),
        name="scores",
    )(*held([spread]))


def rows_of(a):
    years, _, slots, channels, grid = a.shape
    t = a.reshape(years, slots, channels, grid // LANES, LANES).transpose(0, 2, 3, 1, 4)
    return t.reshape(years, channels * (grid // LANES) * slots, LANES)


def latitude_weight(pixel):
    return jnp.cos((pixel % 181 - 90).astype(jnp.float32) * (math.pi / 180.0))


def step(predicted_anomaly, measured_anomaly, filled_calendar):
    hindcast, _, slots, channels, grid = predicted_anomaly.shape
    n_year, n_date, n_pix = lax.axis_size("year"), lax.axis_size("date"), lax.axis_size("pix")
    chips = n_year // CORES
    tiles = grid // (LANES * n_year * n_date)
    year, date, pix = lax.axis_index("year"), lax.axis_index("date"), lax.axis_index("pix")
    where = filled_calendar
    f_rows, o_rows = rows_of(predicted_anomaly), rows_of(measured_anomaly)
    swap = [(y, y // CORES * CORES + (y + 1) % CORES) for y in range(n_year)]
    scale = float(hindcast * n_year)

    def hop(a, k):
        return lax.ppermute(a, "year", [(y, (y + k * CORES) % n_year) for y in range(n_year)])

    def halve(stay, leave):
        got, k, half = [], 1, n_date // 2
        while half:
            got.append(lax.ppermute(leave, "date", [(d, d ^ k) for d in range(n_date)]))
            k, half = 2 * k, half // 2
            if half:
                leave = stay[half : 2 * half] + sum(g[half : 2 * half] for g in got)
        return [stay, *got]

    edges = (0, *SPLITS, channels)
    spans = list(zip(edges[:-1], edges[1:]))
    last = len(spans) - 1
    rests, leaving, after = [], [], []
    for q, (first, end) in enumerate(spans):
        rows = ((end - first) * tiles + 7) // 8 * 8
        away, rest, away_send, rest_send = moments(
            where, f_rows, o_rows, after, first, end - first, rows, KINDS[q], chips, n_date, tiles, slots
        )
        away_got = lax.ppermute(away_send, "year", swap)
        rests.append((rest, lax.ppermute(rest_send, "year", swap)))
        after = [away[:, :, k] + away_got[:, :, k] for k in range(chips - 1)]
        leaving.append(after)
    biases, parts = [], []
    for q, (rest, rest_got) in enumerate(rests):
        arrived = [hop(a, k + 1) for k, a in enumerate(leaving[q])]
        stay, leave, bias = corrected(where, scale, KINDS[q], rest, rest_got, arrived)
        biases.append(bias)
        parts.append(halve(stay, leave))
    segments, at = {}, 0
    for q in range(last):
        for field in range(KINDS[q], FIELDS):
            segments[(q, field)] = (at, rests[q][0].shape[2])
            at += rests[q][0].shape[2]
    group = rests[: max(q for q, _ in segments) + 1]
    z_parts = halve(*observed(where, chips, segments, KINDS, group))
    x_parts = [sum(p[0, k] for p in z_parts) for k in range(1, chips)]
    x_parts = [hop(a, k + 1) for k, a in enumerate(x_parts)]

    start = pix * grid + (year * n_date + date) * (tiles * LANES)
    row = jnp.arange(8, dtype=jnp.int32)[:, None] % tiles
    weight = latitude_weight(start + row * LANES + jnp.arange(LANES, dtype=jnp.int32)[None, :])
    weight_total = jnp.sum(latitude_weight(jnp.arange(n_pix * grid, dtype=jnp.int32)))
    weight = jnp.concatenate([weight, jnp.broadcast_to(weight_total, (8, LANES))], axis=0)
    n, n_early = channels * tiles, SPLITS[-1] * tiles
    reach = n_early + parts[last][0].shape[2]
    pick = jnp.arange(reach, dtype=jnp.int32)[:, None] // tiles
    pick = (pick == jnp.arange(LANES, dtype=jnp.int32)[None, :]).astype(jnp.float32)
    rows = [p[0].shape[2] for p in parts[:last]]
    acc_early, rmse_early, sums = maps_call(
        functools.partial(early_kernel, scale, rows, segments, len(z_parts)),
        n_early,
        (8, LANES),
        [weight, pick, *(a for p in parts[:last] for a in p), *z_parts, *x_parts],
    )
    acc_last, rmse_last, part = maps_call(
        functools.partial(last_kernel, n_early, n),
        n - n_early,
        (n_year * n_date * n_pix, 2, LANES),
        [weight, pick, sums, *parts[last]],
    )
    acc = jnp.concatenate([acc_early, acc_last], axis=0)
    rmse = jnp.concatenate([rmse_early, rmse_last], axis=0)
    spread = lax.all_to_all(part, ("year", "date", "pix"), 0, 0, tiled=True)
    scores = scores_of(spread, channels)

    cut = [b[:, : (end - first) * tiles] for b, (first, end) in zip(biases, spans)]
    bias = jnp.concatenate(cut, axis=1).reshape(n_date, channels, tiles, LANES).transpose(1, 0, 2, 3)
    flat = (channels, 1, tiles * LANES)
    return (bias.reshape(1, channels, 1, -1), acc.reshape(flat), rmse.reshape(flat), scores)


def solution(mesh):
    placed = (P("year", "date", None, None, "pix"), P("year", "date", None, None, "pix"), P("date"))
    return jax.shard_map(
        step,
        mesh=mesh,
        in_specs=placed,
        out_specs=(
            P("date", None, "pix", "year"),
            P(None, "pix", ("year", "date")),
            P(None, "pix", ("year", "date")),
            P(),
        ),
        check_vma=False,
    )
```
